32 devices in a mesh: seq: 8 (over z, y), kvh: 4 (over x, core).
Axes of the slice: x: 2, y: 2, z: 4, core: 2. Of those that a mesh axis runs over, the one named last changes fastest.
Arguments:
- queries: bfloat16 [2048, 4096], P(('seq', 'kvh')), may hold values from -8 to 8
- keys: bfloat16 [2048, 2048], P(('seq', 'kvh')), may hold values from -8 to 8
- values: bfloat16 [2048, 2048], P(('seq', 'kvh')), may hold values from -6 to 6
- out_grad: bfloat16 [2048, 4096], P(('seq', 'kvh')), may hold values from -6 to 6
- file_start: int32 [2048], P('seq'), may hold values from 0 to 2047, as said below
Outputs:
- attn_out: bfloat16 [2048, 4096], P(('seq', 'kvh'))
- query_grad: bfloat16 [2048, 4096], P(('seq', 'kvh'))
- key_gradient: bfloat16 [2048, 2048], P(('seq', 'kvh'))
- value_gradient: bfloat16 [2048, 2048], P(('seq', 'kvh'))
The draws below stay inside these ranges and needn't reach their ends.
Inputs may be any that keep to these rules, and one draw needn't show every extreme that they name: `file_start`: entries never fall along the slab; each entry is at most its own token's position, and equals it at the first token of a file; the first file starts at 0 and the slab's last token begins a file of its own.
All inputs are finite; a program needn't handle non-finite values.
Results may differ from the reference program's by a relative error of at most 0.024.
Values may be sent and summed in bfloat16 or wider, within the bound.
A program may use at most 128 MiB of HBM per device.

```python
import math
import jax
import jax.numpy as jnp
from jax import lax

QUERY_HEADS = 32
KEY_VALUE_HEADS = 16
HEAD_SIZE = 128
WINDOW_TOKENS = 1024
SLAB_TOKENS = 2048


def file_starts(key):
    lengths = jax.random.randint(jax.random.fold_in(key, 11), (SLAB_TOKENS // 2 + 1,), 2, 3 * WINDOW_TOKENS + 1, dtype=jnp.int32)
    file_ends = jnp.cumsum(lengths).astype(jnp.int32)
    begins = file_ends - lengths
    positions = jnp.arange(SLAB_TOKENS, dtype=jnp.int32)
    file_index = jnp.searchsorted(file_ends, positions, side='right')
    starts = begins[file_index].astype(jnp.int32)
    return jnp.where(positions == SLAB_TOKENS - 1, positions, starts).astype(jnp.int32)


def drawn(key):
    starting_key = jax.random.fold_in(key, 5)
    query_key = jax.random.fold_in(starting_key, 1)
    key_random_seed = jax.random.fold_in(starting_key, 2)
    query_vals = jnp.clip(1.6 * jax.random.normal(query_key, (SLAB_TOKENS, QUERY_HEADS * HEAD_SIZE), jnp.float32), -8.0, 8.0)
    key_entries = jnp.clip(1.6 * jax.random.normal(key_random_seed, (SLAB_TOKENS, KEY_VALUE_HEADS * HEAD_SIZE), jnp.float32), -8.0, 8.0)
    return (query_vals, key_entries)


def draw_queries(key, part):
    return drawn(key)[0].astype(jnp.bfloat16)


def draw_keys(key, part):
    return drawn(key)[1].astype(jnp.bfloat16)


def draw_file_start(key, part):
    return file_starts(key)


def levels(key, dims, cuts, least, high):
    def one(dim, shards_of):
        steps = jax.random.uniform(jax.random.fold_in(jax.random.fold_in(key, 6), dim), (shards_of,), jnp.float32, least / len(cuts), high / len(cuts))
        return jnp.repeat(jnp.exp(steps), dims[dim] // shards_of).reshape((-1,) + (1,) * (len(dims) - dim - 1))

    level = one(*cuts[0])
    for cut in cuts[1:]:
        level = level * one(*cut)
    return level


def gaussian(stream_key, dims, scale, bound, cuts=(), held_as=jnp.bfloat16):
    result = jax.random.normal(stream_key, dims, jnp.float32) * scale
    if len(cuts) > 0:
        result = levels(stream_key, dims, cuts, -0.22, 0.18) * result
    return jnp.clip(result, min=-bound, max=bound).astype(held_as)


def setup_inputs(seed: int = 0) -> dict:
    key_of = jax.random.split(jax.random.key(seed), 6)
    return {
        "queries": draw_queries(jax.random.fold_in(key_of[5], 71), 0),
        "keys": draw_keys(jax.random.fold_in(key_of[5], 71), 0),
        "values": gaussian(key_of[2], (SLAB_TOKENS, KEY_VALUE_HEADS * HEAD_SIZE), 1.0, 6.0, ((0, 32),)),
        "out_grad": gaussian(key_of[3], (SLAB_TOKENS, QUERY_HEADS * HEAD_SIZE), 1.0, 6.0, ((0, 32),)),
        "file_start": draw_file_start(jax.random.fold_in(key_of[5], 71), 0),
    }


score_scale = 168.0 ** -0.5


def reference(queries, keys, values, out_grad, file_start):
    block_rows = math.gcd(SLAB_TOKENS, 512)
    key_extent = block_rows + WINDOW_TOKENS
    group_width = QUERY_HEADS // KEY_VALUE_HEADS
    leading_keys = jnp.concatenate([jnp.zeros((WINDOW_TOKENS, KEY_VALUE_HEADS * HEAD_SIZE), keys.dtype), keys], axis=0).reshape(WINDOW_TOKENS + SLAB_TOKENS, KEY_VALUE_HEADS, HEAD_SIZE)
    leading_values = jnp.concatenate([jnp.zeros((WINDOW_TOKENS, KEY_VALUE_HEADS * HEAD_SIZE), values.dtype), values], axis=0).reshape(WINDOW_TOKENS + SLAB_TOKENS, KEY_VALUE_HEADS, HEAD_SIZE)
    query_all = queries.reshape(SLAB_TOKENS, QUERY_HEADS, HEAD_SIZE)
    grad_all = out_grad.reshape(SLAB_TOKENS, QUERY_HEADS, HEAD_SIZE)
    span_offsets = jnp.arange(key_extent, dtype=jnp.int32)
    row_offsets = jnp.arange(block_rows, dtype=jnp.int32)

    def one_block(carry, block_index):
        key_running_sum, value_running_sum = carry
        start_row = (block_index * block_rows).astype(jnp.int32)
        query_block = lax.dynamic_slice_in_dim(query_all, start_row, block_rows, 0).astype(jnp.float32)
        grad_block = lax.dynamic_slice_in_dim(grad_all, start_row, block_rows, 0).astype(jnp.float32)
        key_window = lax.dynamic_slice_in_dim(leading_keys, start_row, key_extent, 0).astype(jnp.float32)
        value_window = lax.dynamic_slice_in_dim(leading_values, start_row, key_extent, 0).astype(jnp.float32)
        file_begins = lax.dynamic_slice_in_dim(file_start, start_row, block_rows, 0)
        query_pos = start_row + row_offsets
        key_pos = start_row - WINDOW_TOKENS + span_offsets
        lower_key = jnp.maximum(file_begins, query_pos - WINDOW_TOKENS + 1)
        allowed = (key_pos[None, :] >= lower_key[:, None]) & (key_pos[None, :] <= query_pos[:, None])
        key_rep = jnp.repeat(key_window, group_width, axis=1)
        value_rep = jnp.repeat(value_window, group_width, axis=1)
        scores = jnp.einsum("qhd,khd->hqk", query_block, key_rep) * score_scale
        scores = jnp.where(allowed[None], scores, -jnp.inf)
        row_peak = jnp.max(scores, axis=2, keepdims=True)
        log_total = row_peak + jnp.log(jnp.sum(jnp.exp(scores - row_peak), axis=2, keepdims=True))
        prob_full = jnp.exp(scores - log_total)
        prob_low = lax.optimization_barrier(prob_full.astype(jnp.bfloat16)).astype(jnp.float32)
        attention = jnp.einsum("hqk,khd->qhd", prob_low, value_rep).astype(jnp.bfloat16)
        row_delta = jnp.transpose(jnp.sum(grad_block * attention.astype(jnp.float32), axis=2))
        prob_grad = jnp.einsum("qhd,khd->hqk", grad_block, value_rep)
        score_grad = lax.optimization_barrier((prob_full * (prob_grad - row_delta[:, :, None])).astype(jnp.bfloat16)).astype(jnp.float32)
        query_grad = (score_scale * jnp.einsum("hqk,khd->qhd", score_grad, key_rep)).astype(jnp.bfloat16)
        key_portion = score_scale * jnp.einsum("hqk,qhd->khd", score_grad, query_block)
        key_portion = key_portion.reshape(key_extent, KEY_VALUE_HEADS, group_width, HEAD_SIZE).sum(axis=2)
        value_portion = jnp.einsum("hqk,qhd->khd", prob_low, grad_block)
        value_portion = value_portion.reshape(key_extent, KEY_VALUE_HEADS, group_width, HEAD_SIZE).sum(axis=2)
        key_running_sum = lax.dynamic_update_slice_in_dim(key_running_sum, lax.dynamic_slice_in_dim(key_running_sum, start_row, key_extent, 0) + key_portion, start_row, 0)
        value_running_sum = lax.dynamic_update_slice_in_dim(value_running_sum, lax.dynamic_slice_in_dim(value_running_sum, start_row, key_extent, 0) + value_portion, start_row, 0)
        return (key_running_sum, value_running_sum), (attention.reshape(block_rows, QUERY_HEADS * HEAD_SIZE), query_grad.reshape(block_rows, QUERY_HEADS * HEAD_SIZE))

    empty_running_sum = jnp.zeros((WINDOW_TOKENS + SLAB_TOKENS, KEY_VALUE_HEADS, HEAD_SIZE), jnp.float32)
    block_ids = jnp.arange(SLAB_TOKENS // block_rows, dtype=jnp.int32)
    (key_running_sum, value_running_sum), (attention, query_grad) = lax.scan(one_block, (empty_running_sum, empty_running_sum), block_ids)
    attn_out = attention.reshape(SLAB_TOKENS, QUERY_HEADS * HEAD_SIZE)
    query_grad = query_grad.reshape(SLAB_TOKENS, QUERY_HEADS * HEAD_SIZE)
    key_gradient = key_running_sum[WINDOW_TOKENS:].reshape(SLAB_TOKENS, KEY_VALUE_HEADS * HEAD_SIZE).astype(jnp.bfloat16)
    value_gradient = value_running_sum[WINDOW_TOKENS:].reshape(SLAB_TOKENS, KEY_VALUE_HEADS * HEAD_SIZE).astype(jnp.bfloat16)
    return (attn_out, query_grad, key_gradient, value_gradient)
```

```python
import functools
import math

import jax
import jax.numpy as jnp
from jax import lax
from jax.experimental import pallas as pl
from jax.experimental.pallas import tpu as pltpu
from jax.sharding import PartitionSpec as P

HEAD_SIZE = 128
WINDOW_TOKENS = 1024
SCALE = 168.0 ** (-0.5)
EXP2_SCALE = SCALE / math.log(2.0)
MASKED = -1e30
MESH = pl.DeviceIdType.MESH

NT = (((1,), (1,)), ((), ()))
NN = (((1,), (0,)), ((), ()))
TN = (((0,), (0,)), ((), ()))

K, V, Q, G = range(4)
ATTN, DQ, DK, DV = range(4)


def matmul(left, right, dims):
    return lax.dot_general(left, right, dims, preferred_element_type=jnp.float32)


def kernel(
    seq_count, kvh_count, kv_local, group, rows,
    k_in, v_in, q_in, g_in, starts_in,
    attn_out, dq_out, dk_out, dv_out, dk_later, dv_later,
    win, qg, starts, scores, probs, out_t, ghat, delta, dq_t, attn_buf, dq_buf,
    part, grad_send, grad_recv, dkv_low, blank,
    in_send, in_recv, start_send, start_recv, own_send, own_recv, far_send, far_recv,
    far_grad_send, far_grad_recv, near_send, near_recv, out_send, out_recv,
):
    ranks = 2 * kvh_count
    piece = rows // kvh_count
    tokens = 2 * rows
    width = group * HEAD_SIZE
    spread_rows = group * rows
    seq = lax.axis_index("seq")
    me = lax.axis_index("kvh")
    odd = lax.rem(seq, 2)
    shard = seq // 2
    shards = seq_count // 2
    rank = odd * kvh_count + me
    has_next = shard + 1 < shards
    has_previous = shard >= 1
    behind_two = shard >= 2

    def peer(off):
        found = 0
        bit = 1
        while bit < ranks:
            mine = lax.rem(rank // bit, 2)
            found = found + (1 - mine if off & bit else mine) * bit
            bit *= 2
        return found

    def place(other, there=shard):
        return (2 * there + other // kvh_count, lax.rem(other, kvh_count))

    offs = sorted(range(1, ranks), key=lambda off: (off == 1, off & 1, off))

    bases = range(2, ranks, 2)
    side = lax.rem(rank, 2)

    barrier = pltpu.get_barrier_semaphore()
    for off in offs:
        pl.semaphore_signal(barrier, inc=1, device_id=place(peer(off)), device_id_type=MESH)

    @pl.when(has_next)
    def _():
        for other in range(ranks):
            pl.semaphore_signal(
                barrier, inc=1, device_id=place(other, shard + 1), device_id_type=MESH
            )

    @pl.when(has_previous)
    def _():
        pl.semaphore_signal(barrier, inc=1, device_id=(seq - 2, me), device_id_type=MESH)

    @pl.when(jnp.logical_not(behind_two))
    def _():
        win[2] = jnp.zeros_like(win[2])

    @pl.when(jnp.logical_not(has_previous))
    def _():
        win[1] = jnp.zeros_like(win[1])

    pl.semaphore_wait(
        barrier,
        ranks - 1 + has_next.astype(jnp.int32) + ranks * has_previous.astype(jnp.int32),
    )

    sources = (k_in, v_in, q_in, g_in)
    widths = (HEAD_SIZE, HEAD_SIZE, width, width)
    targets = (attn_out, dq_out, dk_out, dv_out)
    out_widths = (width, width, HEAD_SIZE, HEAD_SIZE)

    def in_source(kind, head, owner):
        start = pl.multiple_of((owner * kv_local + head) * widths[kind], 128)
        return sources[kind].at[:, pl.ds(start, widths[kind])]

    def in_buffer(kind, head):
        return win.at[0, head, kind] if kind < 2 else qg.at[kind - 2, head]

    def in_target(kind, head):
        block = pl.ds(pl.multiple_of(rank * piece, piece), piece)
        if kind < 2:
            return win.at[0, head, kind, block, :]
        return qg.at[kind - 2, head, block, :]

    def in_copy(kind, head, base, core):
        other = peer(base) - side + core
        return pltpu.make_async_remote_copy(
            src_ref=in_source(kind, head, other),
            dst_ref=in_target(kind, head),
            send_sem=in_send.at[kind, head, base + core],
            recv_sem=in_recv.at[kind, head],
            device_id=place(other),
            device_id_type=MESH,
        )

    def in_own(kind, head):
        return pltpu.make_async_copy(
            in_source(kind, head, rank), in_target(kind, head), in_recv.at[kind, head]
        )

    def in_start(kind, head, core):
        for base in bases:
            in_copy(kind, head, base, core).start()

        @pl.when(side != core)
        def _():
            in_copy(kind, head, 0, core).start()

        @pl.when(side == core)
        def _():
            in_own(kind, head).start()

    def in_wait(kind, head):
        whole = in_buffer(kind, head)
        pltpu.make_async_copy(whole, whole, in_recv.at[kind, head]).wait()

    def start_copy():
        return pltpu.make_async_remote_copy(
            src_ref=starts_in,
            dst_ref=starts.at[odd],
            send_sem=start_send,
            recv_sem=start_recv,
            device_id=(seq + 1 - 2 * odd, me),
            device_id_type=MESH,
        )

    def hop(level, kind, head):
        send, recv = ((own_send, own_recv), (far_send, far_recv))[level]
        return pltpu.make_async_remote_copy(
            src_ref=win.at[level, head, kind],
            dst_ref=win.at[level + 1, head, kind],
            send_sem=send.at[head, kind],
            recv_sem=recv.at[head, kind],
            device_id=(seq + 2, me),
            device_id_type=MESH,
        )

    def send_own(head, kinds=(K, V)):
        for kind in kinds:
            in_wait(kind, head)

            @pl.when(has_next)
            def _():
                hop(0, kind, head).start()

    def pass_on(head):
        @pl.when(has_previous)
        def _():
            for kind in (K, V):
                hop(0, kind, head).wait_recv()

                @pl.when(has_next)
                def _(kind=kind):
                    hop(1, kind, head).start()

    def wait_far(head, kind):
        @pl.when(behind_two)
        def _():
            hop(1, kind, head).wait_recv()

    def far_grad_copy(head, half):
        return pltpu.make_async_remote_copy(
            src_ref=grad_send.at[1, head, half],
            dst_ref=grad_recv.at[head, half],
            send_sem=far_grad_send.at[head, half],
            recv_sem=far_grad_recv.at[head, half],
            device_id=(seq - 2, me),
            device_id_type=MESH,
        )

    later = (dk_later, dv_later)

    def near_start(head, half):
        start = pl.multiple_of((rank * kv_local + head) * HEAD_SIZE, 128)
        for i in range(kvh_count):
            for kind in range(2):
                pltpu.make_async_remote_copy(
                    src_ref=grad_send.at[0, head, half, kind, i * piece : (i + 1) * piece, :],
                    dst_ref=later[kind].at[:, pl.ds(start, HEAD_SIZE)],
                    send_sem=near_send.at[head, half],
                    recv_sem=near_recv.at[kind],
                    device_id=(2 * (shard - 1) + half, i),
                    device_id_type=MESH,
                ).start()

    def out_source(kind, head, owner):
        if kind < 2:
            block = pl.ds(pl.multiple_of(owner * piece, piece), piece)
            return (attn_buf, dq_buf)[kind].at[head, block, :]
        block = pl.ds(pl.multiple_of(lax.rem(owner, kvh_count) * piece, piece), piece)
        return dkv_low.at[head, owner // kvh_count, kind - 2, block, :]

    def out_target(kind, head):
        start = pl.multiple_of((rank * kv_local + head) * out_widths[kind], 128)
        return targets[kind].at[:, pl.ds(start, out_widths[kind])]

    def out_copy(kind, head, off):
        other = peer(off)
        return pltpu.make_async_remote_copy(
            src_ref=out_source(kind, head, other),
            dst_ref=out_target(kind, head),
            send_sem=out_send.at[kind, head, off - 1],
            recv_sem=out_recv.at[kind],
            device_id=place(other),
            device_id_type=MESH,
        )

    def out_start(kinds, head, half):
        @pl.when(odd == half)
        def _():
            for kind in kinds:
                for off in offs:
                    if off < kvh_count:
                        out_copy(kind, head, off).start()
                pltpu.make_async_copy(
                    out_source(kind, head, rank), out_target(kind, head), out_recv.at[kind]
                ).start()

        @pl.when(odd != half)
        def _():
            for kind in kinds:
                for off in offs:
                    if off >= kvh_count:
                        out_copy(kind, head, off).start()

    blocks = WINDOW_TOKENS // rows + 1

    def keys(kind, head, b):
        return win[2 - b // 2, head, kind, (b % 2) * rows : (b % 2 + 1) * rows, :]

    def stacked(kind, head, s):
        wide = qg[kind - 2, head, s * rows : (s + 1) * rows, :]
        return jnp.concatenate(
            [wide[:, i * HEAD_SIZE : (i + 1) * HEAD_SIZE] for i in range(group)], axis=0
        )

    def put(buffer, head, s, tall):
        for i in range(group):
            buffer[head, s * rows : (s + 1) * rows, i * HEAD_SIZE : (i + 1) * HEAD_SIZE] = tall[
                i * rows : (i + 1) * rows
            ]

    row_pos = lax.broadcasted_iota(jnp.int32, (1, rows), 1)
    position = jnp.concatenate([row_pos] * group, axis=1)
    spots = lax.broadcasted_iota(jnp.int32, (rows, spread_rows), 0)

    def score(head, s, bs, peak):
        queries = stacked(Q, head, s)
        low = jnp.maximum(starts[s] - (seq - odd + s) * rows, row_pos - (WINDOW_TOKENS - 1))
        low = jnp.concatenate([low] * group, axis=1)
        for b in bs:
            j = b - s
            raw = matmul(keys(K, head, b), queries, NT)
            spot = spots + (j - (blocks - 1)) * rows
            allowed = spot >= low
            if j == blocks - 1:
                allowed = jnp.logical_and(allowed, spots <= position)
            raw = jnp.where(allowed, raw, MASKED)
            scores[head, s, j] = raw
            top = jnp.max(raw, axis=0, keepdims=True)
            peak = top if peak is None else jnp.maximum(peak, top)
        return peak

    def attend(head, s, peak):
        total = None
        out = None
        for j in range(blocks):
            raised = jnp.exp2((scores[head, s, j] - peak) * EXP2_SCALE)
            low = raised.astype(jnp.bfloat16)
            probs[s, j] = low
            term = matmul(keys(V, head, j + s), low, TN)
            out = term if out is None else out + term
            bit = jnp.sum(raised, axis=0, keepdims=True)
            total = bit if total is None else total + bit
        inverse = 1.0 / total
        attention = (out * inverse).astype(jnp.bfloat16).astype(jnp.float32)
        put(attn_buf, head, s, jnp.transpose(attention).astype(jnp.bfloat16))
        out_start((ATTN,), head, s)
        grads_t = jnp.transpose(stacked(G, head, s).astype(jnp.float32)) * inverse
        delta[s] = jnp.sum(grads_t * attention, axis=0, keepdims=True)
        ghat[s] = jnp.transpose(grads_t).astype(jnp.bfloat16)

    def backward(head, b):
        key_part = None
        value_part = None
        for s in range(2):
            j = b - s
            if j < 0 or j >= blocks:
                continue
            low = probs[s, j]
            grads = ghat[s]
            prob_grad = matmul(keys(V, head, b), grads, NT)
            score_grad = (low.astype(jnp.float32) * (prob_grad - delta[s])).astype(jnp.bfloat16)
            value_term = matmul(low, grads, NN)
            key_term = matmul(score_grad, stacked(Q, head, s), NN)
            key_part = key_term if key_part is None else key_part + key_term
            value_part = value_term if value_part is None else value_part + value_term
            query_term = matmul(keys(K, head, b), score_grad, TN)
            if j == 0:
                dq_t[s] = query_term
            else:
                dq_t[s] += query_term
        return key_part * SCALE, value_part

    def far_grads(head):
        for half in range(2):
            key_part, value_part = backward(head, half)
            grad_send[1, head, half, 0] = key_part.astype(jnp.bfloat16)
            grad_send[1, head, half, 1] = value_part.astype(jnp.bfloat16)

            @pl.when(behind_two)
            def _(half=half):
                far_grad_copy(head, half).start()

    def near_grads(head):
        for half in range(2):
            key_part, value_part = backward(head, 2 + half)
            part[head, half, 0] = key_part
            part[head, half, 1] = value_part

    def own_grads(head):
        for half in range(2):
            key_part, value_part = backward(head, 4 + half)
            dkv_low[head, half, 0] = key_part.astype(jnp.bfloat16)
            dkv_low[head, half, 1] = value_part.astype(jnp.bfloat16)
        for s in range(2):
            put(dq_buf, head, s, jnp.transpose(dq_t[s] * SCALE).astype(jnp.bfloat16))
            out_start((DQ,), head, s)
        for half in range(2):
            out_start((DK, DV), head, half)

    def collect_near(head):
        for half in range(2):

            @pl.when(jnp.logical_and(has_previous, has_next))
            def _(half=half):
                far_grad_copy(head, half).wait_recv()
                part[head, half] += grad_recv[head, half].astype(jnp.float32)

            @pl.when(has_previous)
            def _(half=half):
                grad_send[0, head, half] = part[head, half].astype(jnp.bfloat16)
                near_start(head, half)

    start_copy().start()
    starts[odd] = starts_in[...]
    for head in range(kv_local):
        for kinds in ((K, V), (Q, G)):
            for core in range(2):
                for kind in kinds:
                    in_start(kind, head, core)

    @pl.when(jnp.logical_not(has_next))
    def _():
        blank[...] = jnp.zeros_like(blank)
        for kind in range(2):
            pltpu.make_async_copy(blank, later[kind], near_recv.at[kind]).start()

    start_copy().wait_recv()

    peaks = {}

    def score_own(head):
        for s in range(2):
            peaks[head, s] = score(head, s, range(4 + s, 3, -1), None)

    def score_near(head):
        for s in range(2):
            peaks[head, s] = score(head, s, (2, 3), peaks[head, s])

    def score_far(head):
        for s in range(2):
            peaks[head, s] = score(head, s, range(s, 2), peaks[head, s])

    send_own(0)
    pass_on(0)
    for head in range(kv_local):
        if head + 1 < kv_local and head == 0:
            send_own(1)
        in_wait(Q, head)
        score_own(head)
        score_near(head)
        if head:
            collect_near(head - 1)
        wait_far(head, K)
        score_far(head)
        wait_far(head, V)
        in_wait(G, head)
        for s in range(2):
            attend(head, s, peaks[head, s])
        far_grads(head)
        near_grads(head)
        own_grads(head)
        if head + 1 < kv_local:
            pass_on(head + 1)
            if head + 2 < kv_local:
                send_own(head + 2)
    collect_near(kv_local - 1)

    start_copy().wait_send()
    for head in range(kv_local):
        for kind in range(4):
            for off in offs:
                out_copy(kind, head, off).wait_send()
            for core in range(2):
                for base in bases:
                    in_copy(kind, head, base, core).wait_send()
            in_copy(kind, head, 0, 1 - side).wait_send()
        for kind in (K, V):

            @pl.when(has_next)
            def _(kind=kind, head=head):
                hop(0, kind, head).wait_send()

            @pl.when(jnp.logical_and(has_previous, has_next))
            def _(kind=kind, head=head):
                hop(1, kind, head).wait_send()

        for half in range(2):

            @pl.when(has_previous)
            def _(half=half, head=head):
                sent = grad_send.at[0, head, half]
                pltpu.make_async_copy(sent, sent, near_send.at[head, half]).wait()

            @pl.when(behind_two)
            def _(half=half, head=head):
                far_grad_copy(head, half).wait_send()

    for kind in range(2):
        pltpu.make_async_copy(later[kind], later[kind], near_recv.at[kind]).wait()
    for kind in range(4):
        pltpu.make_async_copy(targets[kind], targets[kind], out_recv.at[kind]).wait()


def finish_kernel(chunks, *refs):
    landed, results = refs[:6], refs[6:10]
    held, sems = refs[-2:]

    def slot(i, block):
        return held.at[i, block, : landed[i].shape[1]]

    loads, stores = [], []
    for i in range(6):
        rows = landed[i].shape[0] // chunks
        for j in range(chunks):
            block = pl.ds(j * rows, rows)
            load = pltpu.make_async_copy(landed[i].at[block], slot(i, block), sems.at[0, i, j])
            load.start()
            loads.append((i, j, block, load))
    for i, j, block, load in loads:
        load.wait()
        if i >= 4:
            width = landed[i].shape[1]
            total = held[i - 2, block, :width].astype(jnp.float32) + held[
                i, block, :width
            ].astype(jnp.float32)
            held[i, block, :width] = total.astype(jnp.bfloat16)
        if i < 2 or i >= 4:
            k = i if i < 2 else i - 2
            store = pltpu.make_async_copy(slot(i, block), results[k].at[block], sems.at[1, k, j])
            store.start()
            stores.append(store)
    for store in stores:
        store.wait()


def body(seq_count, kvh_count, queries, keys, values, out_grad, file_start):
    rows = file_start.shape[0]
    kv_local = keys.shape[1] // (HEAD_SIZE * 2 * kvh_count)
    group = queries.shape[1] // keys.shape[1]
    bf16, f32 = jnp.bfloat16, jnp.float32
    width = group * HEAD_SIZE
    tokens = 2 * rows
    wide = group * rows
    blocks = WINDOW_TOKENS // rows + 1
    dma = pltpu.SemaphoreType.DMA
    anywhere = pl.BlockSpec(memory_space=pl.ANY)
    vmem = pl.BlockSpec(memory_space=pltpu.VMEM)
    shapes = tuple(
        jax.ShapeDtypeStruct(like.shape, bf16) for like in (queries, queries, keys, values)
    )
    later = (shapes[2], shapes[3])
    landed = pl.pallas_call(
        functools.partial(kernel, seq_count, kvh_count, kv_local, group, rows),
        out_shape=shapes + later,
        in_specs=[anywhere] * 4 + [vmem],
        out_specs=(anywhere,) * 6,
        scratch_shapes=[
            pltpu.VMEM((3, kv_local, 2, tokens, HEAD_SIZE), bf16),
            pltpu.VMEM((2, kv_local, tokens, width), bf16),
            pltpu.VMEM((2, 1, rows), jnp.int32),
            pltpu.VMEM((kv_local, 2, blocks, rows, wide), f32),
            pltpu.VMEM((2, blocks, rows, wide), bf16),
            pltpu.VMEM((2, HEAD_SIZE, wide), f32),
            pltpu.VMEM((2, wide, HEAD_SIZE), bf16),
            pltpu.VMEM((2, 1, wide), f32),
            pltpu.VMEM((2, HEAD_SIZE, wide), f32),
            pltpu.VMEM((kv_local, tokens, width), bf16),
            pltpu.VMEM((kv_local, tokens, width), bf16),
            pltpu.VMEM((kv_local, 2, 2, rows, HEAD_SIZE), f32),
            pltpu.VMEM((2, kv_local, 2, 2, rows, HEAD_SIZE), bf16),
            pltpu.VMEM((kv_local, 2, 2, rows, HEAD_SIZE), bf16),
            pltpu.VMEM((kv_local, 2, 2, rows, HEAD_SIZE), bf16),
            pltpu.VMEM(keys.shape, bf16),
            dma((4, kv_local, 2 * kvh_count)),
            dma((4, kv_local)),
            dma,
            dma,
            dma((kv_local, 2)),
            dma((kv_local, 2)),
            dma((kv_local, 2)),
            dma((kv_local, 2)),
            dma((kv_local, 2)),
            dma((kv_local, 2)),
            dma((kv_local, 2)),
            dma((2,)),
            dma((4, kv_local, 2 * kvh_count - 1)),
            dma((4,)),
        ],
        compiler_params=pltpu.CompilerParams(
            collective_id=0, has_side_effects=True, vmem_limit_bytes=56 * 1024 * 1024
        ),
    )(keys, values, queries, out_grad, file_start.reshape(1, rows))
    return pl.pallas_call(
        functools.partial(finish_kernel, 2),
        out_shape=shapes,
        in_specs=[anywhere] * 6,
        out_specs=(anywhere,) * 4,
        scratch_shapes=[pltpu.VMEM((6, *queries.shape), bf16), dma((2, 6, 2))],
    )(*landed)


def solution(mesh):
    token_spec = P(("seq", "kvh"), None)
    return jax.shard_map(
        functools.partial(body, mesh.shape["seq"], mesh.shape["kvh"]),
        mesh=mesh,
        in_specs=(token_spec,) * 4 + (P("seq"),),
        out_specs=(token_spec,) * 4,
        check_vma=False,
    )
```

```python
import functools
import math

import jax
import jax.numpy as jnp
from jax import lax
from jax.experimental import pallas as pl
from jax.experimental.pallas import tpu as pltpu
from jax.sharding import PartitionSpec as P

HEAD_SIZE = 128
WINDOW_TOKENS = 1024
SCALE = 168.0 ** (-0.5)
EXP2_SCALE = SCALE / math.log(2.0)
MASKED = -1e30
MESH = pl.DeviceIdType.MESH

NT = (((1,), (1,)), ((), ()))
NN = (((1,), (0,)), ((), ()))
TN = (((0,), (0,)), ((), ()))

K, V, Q, G = range(4)
ATTN, DQ, DK, DV = range(4)


def matmul(left, right, dims):
    return lax.dot_general(left, right, dims, preferred_element_type=jnp.float32)


def kernel(
    seq_count, kvh_count, kv_local, group, rows,
    k_in, v_in, q_in, g_in, starts_in,
    attn_out, dq_out, dk_out, dv_out, dk_later, dv_later,
    win, qg, starts, scores, probs, out_t, ghat, delta, dq_t, attn_buf, dq_buf,
    part, grad_send, grad_recv, dkv_low, blank,
    in_send, in_recv, close_recv, start_send, start_recv, own_send, own_recv, far_send, far_recv,
    far_grad_send, far_grad_recv, near_send, near_recv, out_send, out_recv,
):
    ranks = 2 * kvh_count
    piece = rows // kvh_count
    tokens = 2 * rows
    width = group * HEAD_SIZE
    spread_rows = group * rows
    seq = lax.axis_index("seq")
    me = lax.axis_index("kvh")
    odd = lax.rem(seq, 2)
    shard = seq // 2
    shards = seq_count // 2
    rank = odd * kvh_count + me
    has_next = shard + 1 < shards
    has_previous = shard >= 1
    behind_two = shard >= 2

    def peer(off):
        found = 0
        bit = 1
        while bit < ranks:
            mine = lax.rem(rank // bit, 2)
            found = found + (1 - mine if off & bit else mine) * bit
            bit *= 2
        return found

    def place(other, there=shard):
        return (2 * there + other // kvh_count, lax.rem(other, kvh_count))

    offs = sorted(range(1, ranks), key=lambda off: (off == 1, off & 1, off))

    bases = range(2, ranks, 2)
    side = lax.rem(rank, 2)

    barrier = pltpu.get_barrier_semaphore()
    for off in offs:
        pl.semaphore_signal(barrier, inc=1, device_id=place(peer(off)), device_id_type=MESH)

    @pl.when(has_next)
    def _():
        for other in range(ranks):
            pl.semaphore_signal(
                barrier, inc=1, device_id=place(other, shard + 1), device_id_type=MESH
            )

    @pl.when(has_previous)
    def _():
        pl.semaphore_signal(barrier, inc=1, device_id=(seq - 2, me), device_id_type=MESH)

    @pl.when(jnp.logical_not(behind_two))
    def _():
        win[2] = jnp.zeros_like(win[2])

    @pl.when(jnp.logical_not(has_previous))
    def _():
        win[1] = jnp.zeros_like(win[1])

    pl.semaphore_wait(
        barrier,
        ranks - 1 + has_next.astype(jnp.int32) + ranks * has_previous.astype(jnp.int32),
    )

    sources = (k_in, v_in, q_in, g_in)
    widths = (HEAD_SIZE, HEAD_SIZE, width, width)
    targets = (attn_out, dq_out, dk_out, dv_out)
    out_widths = (width, width, HEAD_SIZE, HEAD_SIZE)

    def in_source(kind, head, owner):
        start = pl.multiple_of((owner * kv_local + head) * widths[kind], 128)
        return sources[kind].at[:, pl.ds(start, widths[kind])]

    def in_buffer(kind, head):
        return win.at[0, head, kind] if kind < 2 else qg.at[kind - 2, head]

    def in_target(kind, head):
        block = pl.ds(pl.multiple_of(rank * piece, piece), piece)
        if kind < 2:
            return win.at[0, head, kind, block, :]
        return qg.at[kind - 2, head, block, :]

    def in_copy(kind, head, base, core):
        other = peer(base) - side + core
        return pltpu.make_async_remote_copy(
            src_ref=in_source(kind, head, other),
            dst_ref=in_target(kind, head),
            send_sem=in_send.at[kind, head, base + core],
            recv_sem=(in_recv if base else close_recv).at[kind, head],
            device_id=place(other),
            device_id_type=MESH,
        )

    def in_own(kind, head):
        return pltpu.make_async_copy(
            in_source(kind, head, rank), in_target(kind, head), close_recv.at[kind, head]
        )

    def close_start(kind, head, core):
        @pl.when(side != core)
        def _():
            in_copy(kind, head, 0, core).start()

        @pl.when(side == core)
        def _():
            in_own(kind, head).start()

    def in_start(kind, head, core):
        for base in bases:
            in_copy(kind, head, base, core).start()

    def wait_rows(kind, head, sem, count):
        rows_of = in_buffer(kind, head).at[:count, :]
        pltpu.make_async_copy(rows_of, rows_of, sem.at[kind, head]).wait()

    def close_wait(kind, head):
        wait_rows(kind, head, close_recv, 2 * piece)

    def in_wait(kind, head):
        wait_rows(kind, head, in_recv, tokens - 2 * piece)

    def start_copy():
        return pltpu.make_async_remote_copy(
            src_ref=starts_in,
            dst_ref=starts.at[odd],
            send_sem=start_send,
            recv_sem=start_recv,
            device_id=(seq + 1 - 2 * odd, me),
            device_id_type=MESH,
        )

    def hop(level, kind, head):
        send, recv = ((own_send, own_recv), (far_send, far_recv))[level]
        return pltpu.make_async_remote_copy(
            src_ref=win.at[level, head, kind],
            dst_ref=win.at[level + 1, head, kind],
            send_sem=send.at[head, kind],
            recv_sem=recv.at[head, kind],
            device_id=(seq + 2, me),
            device_id_type=MESH,
        )

    def own_part(kind, head, turn):
        block = lax.rem(rank // 2 + turn, kvh_count)
        rows_of = pl.ds(pl.multiple_of(block * 2 * piece, 2 * piece), 2 * piece)
        return pltpu.make_async_remote_copy(
            src_ref=win.at[0, head, kind, rows_of, :],
            dst_ref=win.at[1, head, kind, rows_of, :],
            send_sem=own_send.at[head, kind],
            recv_sem=own_recv.at[head, kind],
            device_id=(seq + 2, me),
            device_id_type=MESH,
        )

    def send_close(head):
        for kind in (K, V):
            close_wait(kind, head)

            @pl.when(has_next)
            def _(kind=kind):
                own_part(kind, head, 0).start()

    def send_own(head):
        for kind in (K, V):
            in_wait(kind, head)

            @pl.when(has_next)
            def _(kind=kind):
                for turn in range(1, kvh_count):
                    own_part(kind, head, turn).start()

    def pass_on(head):
        @pl.when(has_previous)
        def _():
            for kind in (K, V):
                hop(0, kind, head).wait_recv()

                @pl.when(has_next)
                def _(kind=kind):
                    hop(1, kind, head).start()

    def wait_far(head, kind):
        @pl.when(behind_two)
        def _():
            hop(1, kind, head).wait_recv()

    def far_grad_copy(head, half):
        return pltpu.make_async_remote_copy(
            src_ref=grad_send.at[1, head, half],
            dst_ref=grad_recv.at[head, half],
            send_sem=far_grad_send.at[head, half],
            recv_sem=far_grad_recv.at[head, half],
            device_id=(seq - 2, me),
            device_id_type=MESH,
        )

    later = (dk_later, dv_later)

    def near_start(head, half):
        start = pl.multiple_of((rank * kv_local + head) * HEAD_SIZE, 128)
        for i in range(kvh_count):
            for kind in range(2):
                pltpu.make_async_remote_copy(
                    src_ref=grad_send.at[0, head, half, kind, i * piece : (i + 1) * piece, :],
                    dst_ref=later[kind].at[:, pl.ds(start, HEAD_SIZE)],
                    send_sem=near_send.at[head, half],
                    recv_sem=near_recv.at[kind],
                    device_id=(2 * (shard - 1) + half, i),
                    device_id_type=MESH,
                ).start()

    def out_source(kind, head, owner):
        if kind < 2:
            block = pl.ds(pl.multiple_of(owner * piece, piece), piece)
            return (attn_buf, dq_buf)[kind].at[head, block, :]
        block = pl.ds(pl.multiple_of(lax.rem(owner, kvh_count) * piece, piece), piece)
        return dkv_low.at[head, owner // kvh_count, kind - 2, block, :]

    def out_target(kind, head):
        start = pl.multiple_of((rank * kv_local + head) * out_widths[kind], 128)
        return targets[kind].at[:, pl.ds(start, out_widths[kind])]

    def out_copy(kind, head, off):
        other = peer(off)
        return pltpu.make_async_remote_copy(
            src_ref=out_source(kind, head, other),
            dst_ref=out_target(kind, head),
            send_sem=out_send.at[kind, head, off - 1],
            recv_sem=out_recv.at[kind],
            device_id=place(other),
            device_id_type=MESH,
        )

    def out_start(kinds, head, half):
        @pl.when(odd == half)
        def _():
            for kind in kinds:
                for off in offs:
                    if off < kvh_count:
                        out_copy(kind, head, off).start()
                pltpu.make_async_copy(
                    out_source(kind, head, rank), out_target(kind, head), out_recv.at[kind]
                ).start()

        @pl.when(odd != half)
        def _():
            for kind in kinds:
                for off in offs:
                    if off >= kvh_count:
                        out_copy(kind, head, off).start()

    blocks = WINDOW_TOKENS // rows + 1

    def keys(kind, head, b):
        return win[2 - b // 2, head, kind, (b % 2) * rows : (b % 2 + 1) * rows, :]

    def stacked(kind, head, s):
        wide = qg[kind - 2, head, s * rows : (s + 1) * rows, :]
        return jnp.concatenate(
            [wide[:, i * HEAD_SIZE : (i + 1) * HEAD_SIZE] for i in range(group)], axis=0
        )

    def put(buffer, head, s, tall):
        for i in range(group):
            buffer[head, s * rows : (s + 1) * rows, i * HEAD_SIZE : (i + 1) * HEAD_SIZE] = tall[
                i * rows : (i + 1) * rows
            ]

    row_pos = lax.broadcasted_iota(jnp.int32, (1, rows), 1)
    position = jnp.concatenate([row_pos] * group, axis=1)
    spots = lax.broadcasted_iota(jnp.int32, (rows, spread_rows), 0)

    def score(head, s, bs, peak):
        queries = stacked(Q, head, s)
        low = jnp.maximum(starts[s] - (seq - odd + s) * rows, row_pos - (WINDOW_TOKENS - 1))
        low = jnp.concatenate([low] * group, axis=1)
        for b in bs:
            j = b - s
            raw = matmul(keys(K, head, b), queries, NT)
            spot = spots + (j - (blocks - 1)) * rows
            allowed = spot >= low
            if j == blocks - 1:
                allowed = jnp.logical_and(allowed, spots <= position)
            raw = jnp.where(allowed, raw, MASKED)
            scores[head, s, j] = raw
            top = jnp.max(raw, axis=0, keepdims=True)
            peak = top if peak is None else jnp.maximum(peak, top)
        return peak

    def attend(head, s, peak):
        total = None
        out = None
        for j in range(blocks):
            raised = jnp.exp2((scores[head, s, j] - peak) * EXP2_SCALE)
            low = raised.astype(jnp.bfloat16)
            probs[s, j] = low
            term = matmul(keys(V, head, j + s), low, TN)
            out = term if out is None else out + term
            bit = jnp.sum(raised, axis=0, keepdims=True)
            total = bit if total is None else total + bit
        inverse = 1.0 / total
        attention = (out * inverse).astype(jnp.bfloat16).astype(jnp.float32)
        put(attn_buf, head, s, jnp.transpose(attention).astype(jnp.bfloat16))
        out_start((ATTN,), head, s)
        grads_t = jnp.transpose(stacked(G, head, s).astype(jnp.float32)) * inverse
        delta[s] = jnp.sum(grads_t * attention, axis=0, keepdims=True)
        ghat[s] = jnp.transpose(grads_t).astype(jnp.bfloat16)

    def backward(head, b):
        key_part = None
        value_part = None
        for s in range(2):
            j = b - s
            if j < 0 or j >= blocks:
                continue
            low = probs[s, j]
            grads = ghat[s]
            prob_grad = matmul(keys(V, head, b), grads, NT)
            score_grad = (low.astype(jnp.float32) * (prob_grad - delta[s])).astype(jnp.bfloat16)
            value_term = matmul(low, grads, NN)
            key_term = matmul(score_grad, stacked(Q, head, s), NN)
            key_part = key_term if key_part is None else key_part + key_term
            value_part = value_term if value_part is None else value_part + value_term
            query_term = matmul(keys(K, head, b), score_grad, TN)
            if j == 0:
                dq_t[s] = query_term
            else:
                dq_t[s] += query_term
        return key_part * SCALE, value_part

    def far_grads(head):
        for half in range(2):
            key_part, value_part = backward(head, half)
            grad_send[1, head, half, 0] = key_part.astype(jnp.bfloat16)
            grad_send[1, head, half, 1] = value_part.astype(jnp.bfloat16)

            @pl.when(behind_two)
            def _(half=half):
                far_grad_copy(head, half).start()

    def near_grads(head):
        for half in range(2):
            key_part, value_part = backward(head, 2 + half)
            part[head, half, 0] = key_part
            part[head, half, 1] = value_part

    def own_grads(head):
        for half in range(2):
            key_part, value_part = backward(head, 4 + half)
            dkv_low[head, half, 0] = key_part.astype(jnp.bfloat16)
            dkv_low[head, half, 1] = value_part.astype(jnp.bfloat16)
        for s in range(2):
            put(dq_buf, head, s, jnp.transpose(dq_t[s] * SCALE).astype(jnp.bfloat16))
            out_start((DQ,), head, s)
        for half in range(2):
            out_start((DK, DV), head, half)

    def collect_near(head):
        for half in range(2):

            @pl.when(jnp.logical_and(has_previous, has_next))
            def _(half=half):
                far_grad_copy(head, half).wait_recv()
                part[head, half] += grad_recv[head, half].astype(jnp.float32)

            @pl.when(has_previous)
            def _(half=half):
                grad_send[0, head, half] = part[head, half].astype(jnp.bfloat16)
                near_start(head, half)

    start_copy().start()
    starts[odd] = starts_in[...]
    for head in range(kv_local):
        for kinds in ((K, V), (Q, G)):
            for kind in kinds:
                for core in range(2):
                    close_start(kind, head, core)
            for core in range(2):
                for kind in kinds:
                    in_start(kind, head, core)

    @pl.when(jnp.logical_not(has_next))
    def _():
        blank[...] = jnp.zeros_like(blank)
        for kind in range(2):
            pltpu.make_async_copy(blank, later[kind], near_recv.at[kind]).start()

    start_copy().wait_recv()

    peaks = {}

    def score_own(head):
        for s in range(2):
            peaks[head, s] = score(head, s, range(4 + s, 3, -1), None)

    def score_near(head):
        for s in range(2):
            peaks[head, s] = score(head, s, (2, 3), peaks[head, s])

    def score_far(head):
        for s in range(2):
            peaks[head, s] = score(head, s, range(s, 2), peaks[head, s])

    send_close(0)
    send_own(0)
    pass_on(0)
    for head in range(kv_local):
        if head + 1 < kv_local:
            send_close(head + 1)
            send_own(head + 1)
        close_wait(Q, head)
        in_wait(Q, head)
        score_own(head)
        score_near(head)
        if head:
            collect_near(head - 1)
        wait_far(head, K)
        score_far(head)
        wait_far(head, V)
        close_wait(G, head)
        in_wait(G, head)
        for s in range(2):
            attend(head, s, peaks[head, s])
        far_grads(head)
        near_grads(head)
        own_grads(head)
        if head + 1 < kv_local:
            pass_on(head + 1)
    collect_near(kv_local - 1)

    start_copy().wait_send()
    for head in range(kv_local):
        for kind in range(4):
            for off in offs:
                out_copy(kind, head, off).wait_send()
            for core in range(2):
                for base in bases:
                    in_copy(kind, head, base, core).wait_send()
            in_copy(kind, head, 0, 1 - side).wait_send()
        for kind in (K, V):

            @pl.when(has_next)
            def _(kind=kind, head=head):
                hop(0, kind, head).wait_send()

            @pl.when(jnp.logical_and(has_previous, has_next))
            def _(kind=kind, head=head):
                hop(1, kind, head).wait_send()

        for half in range(2):

            @pl.when(has_previous)
            def _(half=half, head=head):
                sent = grad_send.at[0, head, half]
                pltpu.make_async_copy(sent, sent, near_send.at[head, half]).wait()

            @pl.when(behind_two)
            def _(half=half, head=head):
                far_grad_copy(head, half).wait_send()

    for kind in range(2):
        pltpu.make_async_copy(later[kind], later[kind], near_recv.at[kind]).wait()
    for kind in range(4):
        pltpu.make_async_copy(targets[kind], targets[kind], out_recv.at[kind]).wait()


def finish_kernel(chunks, *refs):
    landed, results = refs[:6], refs[6:10]
    held, sems = refs[-2:]

    def slot(i, block):
        return held.at[i, block, : landed[i].shape[1]]

    loads, stores = [], []
    for i in range(6):
        rows = landed[i].shape[0] // chunks
        for j in range(chunks):
            block = pl.ds(j * rows, rows)
            load = pltpu.make_async_copy(landed[i].at[block], slot(i, block), sems.at[0, i, j])
            load.start()
            loads.append((i, j, block, load))
    for i, j, block, load in loads:
        load.wait()
        if i >= 4:
            width = landed[i].shape[1]
            total = held[i - 2, block, :width].astype(jnp.float32) + held[
                i, block, :width
            ].astype(jnp.float32)
            held[i, block, :width] = total.astype(jnp.bfloat16)
        if i < 2 or i >= 4:
            k = i if i < 2 else i - 2
            store = pltpu.make_async_copy(slot(i, block), results[k].at[block], sems.at[1, k, j])
            store.start()
            stores.append(store)
    for store in stores:
        store.wait()


def body(seq_count, kvh_count, queries, keys, values, out_grad, file_start):
    rows = file_start.shape[0]
    kv_local = keys.shape[1] // (HEAD_SIZE * 2 * kvh_count)
    group = queries.shape[1] // keys.shape[1]
    bf16, f32 = jnp.bfloat16, jnp.float32
    width = group * HEAD_SIZE
    tokens = 2 * rows
    wide = group * rows
    blocks = WINDOW_TOKENS // rows + 1
    dma = pltpu.SemaphoreType.DMA
    anywhere = pl.BlockSpec(memory_space=pl.ANY)
    vmem = pl.BlockSpec(memory_space=pltpu.VMEM)
    shapes = tuple(
        jax.ShapeDtypeStruct(like.shape, bf16) for like in (queries, queries, keys, values)
    )
    later = (shapes[2], shapes[3])
    landed = pl.pallas_call(
        functools.partial(kernel, seq_count, kvh_count, kv_local, group, rows),
        out_shape=shapes + later,
        in_specs=[anywhere] * 4 + [vmem],
        out_specs=(anywhere,) * 6,
        scratch_shapes=[
            pltpu.VMEM((3, kv_local, 2, tokens, HEAD_SIZE), bf16),
            pltpu.VMEM((2, kv_local, tokens, width), bf16),
            pltpu.VMEM((2, 1, rows), jnp.int32),
            pltpu.VMEM((kv_local, 2, blocks, rows, wide), f32),
            pltpu.VMEM((2, blocks, rows, wide), bf16),
            pltpu.VMEM((2, HEAD_SIZE, wide), f32),
            pltpu.VMEM((2, wide, HEAD_SIZE), bf16),
            pltpu.VMEM((2, 1, wide), f32),
            pltpu.VMEM((2, HEAD_SIZE, wide), f32),
            pltpu.VMEM((kv_local, tokens, width), bf16),
            pltpu.VMEM((kv_local, tokens, width), bf16),
            pltpu.VMEM((kv_local, 2, 2, rows, HEAD_SIZE), f32),
            pltpu.VMEM((2, kv_local, 2, 2, rows, HEAD_SIZE), bf16),
            pltpu.VMEM((kv_local, 2, 2, rows, HEAD_SIZE), bf16),
            pltpu.VMEM((kv_local, 2, 2, rows, HEAD_SIZE), bf16),
            pltpu.VMEM(keys.shape, bf16),
            dma((4, kv_local, 2 * kvh_count)),
            dma((4, kv_local)),
            dma((4, kv_local)),
            dma,
            dma,
            dma((kv_local, 2)),
            dma((kv_local, 2)),
            dma((kv_local, 2)),
            dma((kv_local, 2)),
            dma((kv_local, 2)),
            dma((kv_local, 2)),
            dma((kv_local, 2)),
            dma((2,)),
            dma((4, kv_local, 2 * kvh_count - 1)),
            dma((4,)),
        ],
        compiler_params=pltpu.CompilerParams(
            collective_id=0, has_side_effects=True, vmem_limit_bytes=56 * 1024 * 1024
        ),
    )(keys, values, queries, out_grad, file_start.reshape(1, rows))
    return pl.pallas_call(
        functools.partial(finish_kernel, 2),
        out_shape=shapes,
        in_specs=[anywhere] * 6,
        out_specs=(anywhere,) * 4,
        scratch_shapes=[pltpu.VMEM((6, *queries.shape), bf16), dma((2, 6, 2))],
    )(*landed)


def solution(mesh):
    token_spec = P(("seq", "kvh"), None)
    return jax.shard_map(
        functools.partial(body, mesh.shape["seq"], mesh.shape["kvh"]),
        mesh=mesh,
        in_specs=(token_spec,) * 4 + (P("seq"),),
        out_specs=(token_spec,) * 4,
        check_vma=False,
    )
```
